32 devices in a mesh: ctx: 4 (over y, core), head: 2 (over x), batch: 4 (over z).
Axes of the slice: x: 2, y: 2, z: 4, core: 2. Of those that a mesh axis runs over, the one named last changes fastest.
Arguments:
- ingest: bfloat16 [4, 4, 12, 128, 4, 256], P('ctx', 'batch', None, None, None, 'head'), may hold values from -6 to 6
- src_shard: int32 [4, 4, 6], P('ctx'), may hold values from 0 to 3, as said below
- src_slot: int32 [4, 4, 6], P('ctx'), may hold values from 0 to 11
- hist_len: int32 [4, 4], P('batch'), may hold values from 1 to 1536, 3072 in all within a row
- w_out: bfloat16 [256, 256], P('head'), may hold values from -0.375 to 0.375
Outputs:
- mixed: bfloat16 [4, 3072, 256], P('batch', 'ctx', 'head')
The draws below stay inside these ranges and needn't reach their ends.
Inputs may be any that keep to these rules, and one draw needn't show every extreme that they name: `src_shard`: for each owner index, every owner's 6 blocks come from exactly two different ingestion shards, 3 from each; no (shard, slot) pair of one owner index feeds two blocks. `hist_len`: the 4 histories of a group fill its 3072 positions in order.
All inputs are finite; a program needn't handle non-finite values.
Results may differ from the reference program's by a relative error of at most 0.0058.
Values may be sent and summed in bfloat16 or wider, within the bound.
A program may use at most 64 MiB of HBM per device.

```python
import math
import jax
import jax.numpy as jnp
import numpy as np
from jax import lax

HD = 128
HEADS = 2
D = 256
BLOCK = 128
BLK_DEV = 6
CAP = 3
GROUPS = 4
CTXS = 4
SLOTS = 12
ROWS_DEV = 768
SEQ = 3072
USERS = 4
HIST_MOST = 1536


def plan_blocks(key):

    def one_ctx(ctx_key):
        key_sources, key_slots, key_order = jax.random.split(ctx_key, 3)
        source_order = jax.vmap(lambda one_key: jax.random.permutation(one_key, GROUPS))(jax.random.split(key_sources, GROUPS))
        sources = source_order[:, :2].astype(jnp.int32)
        requests = sources.reshape(-1)
        request_pos = jnp.arange(2 * GROUPS)
        earlier = (requests[None, :] == requests[:, None]) & (request_pos[None, :] < request_pos[:, None])
        request_rank = jnp.sum(earlier.astype(jnp.int32), axis=1)
        slot_orders = jax.vmap(lambda one_key: jax.random.permutation(one_key, SLOTS))(jax.random.split(key_slots, GROUPS))
        wanted = request_rank[:, None] * CAP + jnp.arange(CAP, dtype=jnp.int32)[None, :]
        chosen_slots = jnp.take_along_axis(slot_orders[requests], wanted, axis=1)
        owner_slots = chosen_slots.reshape(GROUPS, BLK_DEV).astype(jnp.int32)
        owner_shards = jnp.repeat(sources, CAP, axis=1)
        block_order = jax.vmap(lambda one_key: jax.random.permutation(one_key, BLK_DEV))(jax.random.split(key_order, GROUPS))
        return (jnp.take_along_axis(owner_shards, block_order, axis=1), jnp.take_along_axis(owner_slots, block_order, axis=1))
    return jax.vmap(one_ctx)(jax.random.split(jax.random.fold_in(key, 7), CTXS))


def draw_src_shard(key, part):
    return plan_blocks(key)[0].astype(jnp.int32)


def draw_src_slot(key, part):
    return plan_blocks(key)[1].astype(jnp.int32)


def block_scale(own_key, shape, cuts, least, largest):
    def one(axis_at, blocks):
        heights = jax.random.uniform(jax.random.fold_in(jax.random.fold_in(own_key, 6), axis_at), (blocks,), jnp.float32, least / len(cuts), largest / len(cuts))
        return jnp.repeat(jnp.exp(heights), shape[axis_at] // blocks).reshape((-1,) + (1,) * (len(shape) - axis_at - 1))

    gain = one(*cuts[0])
    for cut in cuts[1:]:
        gain = gain * one(*cut)
    return gain


def profile(count, total, most, lean):
    loads = [(1 << 20) // math.isqrt(rank ** lean) + 1 for rank in range(2, count + 1)]
    spare, holding = total - most - (count - 1), [1] * (count - 1)
    while spare > 0:
        free = [i for i in range(count - 1) if holding[i] < most]
        mass, remaining = sum([loads[i] for i in free]), spare
        for i in free:
            addition = min(most - holding[i], max(1, remaining * loads[i] // mass), spare)
            holding[i] = holding[i] + addition
            spare = spare - addition
    return np.array([most] + holding)


def ragged(key, amount, total, most, slope):
    if amount == 2:
        one = jax.random.randint(key, (), max(1, total - most), min(most, total - 1) + 1)
        return jnp.stack([one, total - one])
    sizes = jnp.asarray(profile(amount, total, most, slope), jnp.int32)
    twos = (amount - 1) // 2
    source_of, receiver = sizes[1:1 + 2 * twos:2], sizes[2:2 + 2 * twos:2]
    room = jnp.minimum(source_of - 1, most - receiver)
    shifted = jax.random.randint(jax.random.fold_in(key, 1), (twos,), 0, 1 << 20) % (room + 1)
    sizes = sizes.at[1:1 + 2 * twos:2].set(source_of - shifted).at[2:2 + 2 * twos:2].set(receiver + shifted)
    return sizes[jax.random.permutation(jax.random.fold_in(key, 2), amount)]


def centred(own_key, shape, spread, reach, cuts=(), held_as=jnp.bfloat16):
    loudness = block_scale(own_key, shape, cuts, -0.22, 0.18) if cuts else 1.0
    array = jax.random.normal(own_key, shape, jnp.float32) * spread * loudness
    return jnp.minimum(jnp.maximum(array, -reach), reach).astype(held_as)


def setup_inputs(seed: int = 0) -> dict:
    keys = jax.random.split(jax.random.key(seed), 6)
    return {
        "ingest": centred(keys[0], (CTXS, GROUPS, SLOTS, BLOCK, 4, D), 1.0, 6.0, ((0, 4), (1, 4), (5, 2))),
        "src_shard": draw_src_shard(jax.random.fold_in(keys[5], 71), 0),
        "src_slot": draw_src_slot(jax.random.fold_in(keys[5], 71), 0),
        "hist_len": jax.vmap(lambda own: ragged(own, USERS, SEQ, HIST_MOST, 2))(jax.random.split(keys[3], GROUPS)).reshape((GROUPS, USERS)).astype(jnp.int32),
        "w_out": centred(keys[4], (D, D), D ** -0.5, 0.375, ((0, 2),)),
    }


def reference(ingest, src_shard, src_slot, hist_len, w_out):
    ctx_ids = jnp.arange(CTXS, dtype=jnp.int32)[:, None, None]
    owned = ingest[ctx_ids, src_shard, src_slot]
    owned = jnp.transpose(owned, (1, 0, 2, 3, 4, 5)).reshape(GROUPS, SEQ, 4, HEADS, HD)
    score_scale = 1.0 / math.sqrt(HD)

    def per_group(group_args):
        group_rows, lengths = group_args
        seg_ends = jnp.cumsum(lengths).astype(jnp.int32)
        all_pos = jnp.arange(SEQ, dtype=jnp.int32)
        segment = lax.optimization_barrier(jnp.sum((all_pos[:, None] >= seg_ends[None, :]).astype(jnp.int32), axis=1))
        key_rows = group_rows[:, 1].astype(jnp.float32)
        value_rows = group_rows[:, 2].astype(jnp.float32)

        def per_block(offset):
            query_rows = lax.dynamic_slice_in_dim(group_rows, offset, ROWS_DEV, 0)
            query_pos = offset + jnp.arange(ROWS_DEV, dtype=jnp.int32)
            query_seg = lax.dynamic_slice_in_dim(segment, offset, ROWS_DEV, 0)
            scores = jnp.einsum('qhd,khd->hqk', query_rows[:, 0].astype(jnp.float32), key_rows) * score_scale
            visible = (query_seg[:, None] == segment[None, :]) & (all_pos[None, :] <= query_pos[:, None])
            weights = jnp.where(visible[None], jax.nn.silu(scores), 0.0).astype(jnp.bfloat16)
            weights = lax.optimization_barrier(weights).astype(jnp.float32)
            attended = jnp.einsum('hqk,khd->qhd', weights, value_rows)
            mean_square = lax.optimization_barrier(jnp.mean(attended * attended, axis=-1, keepdims=True))
            normed = attended * lax.rsqrt(mean_square + 1e-06)
            gated = (normed * query_rows[:, 3].astype(jnp.float32)).astype(jnp.bfloat16).reshape(ROWS_DEV, D)
            return jnp.dot(gated, w_out, preferred_element_type=jnp.float32).astype(jnp.bfloat16)
        offsets = jnp.arange(CTXS, dtype=jnp.int32) * ROWS_DEV
        return lax.map(per_block, offsets).reshape(SEQ, D)
    return lax.map(per_group, (owned, hist_len))
```

```python
import functools
import math

import jax
import jax.numpy as jnp
from jax import lax
from jax.experimental import pallas as pl
from jax.experimental.pallas import tpu as pltpu
from jax.sharding import PartitionSpec as P

HD = 128
MESH = pl.DeviceIdType.MESH
QUERY, KEY, VALUE, UPDATE = 0, 1, 2, 3
FIRST_KINDS = (KEY, VALUE, QUERY)


def partner(me, mask, count):
    out = 0
    bit = 1
    while bit < count:
        out = out + lax.rem(lax.div(me, bit) + (mask // bit) % 2, 2) * bit
        bit *= 2
    return out


def kernel(sizes, shard_ref, slot_ref, hist_ref, ingest_ref, w_ref, out_ref,
           send_bufs, send_u, recv_bufs, recv_u, own_k, own_v, own_q, prev_k, prev_v,
           start_ref, att, gated, w_cols, mixed,
           z_send, z_recv, u_send, u_recv, c_send, c_recv, h_send, h_recv, w_send, w_recv):
    groups, ctxs, heads, per_owner, rows = sizes
    capacity = per_owner // 2
    window = ctxs // 2
    row_count = per_owner * rows
    my_group = lax.axis_index("batch")
    my_ctx = lax.axis_index("ctx")
    my_head = lax.axis_index("head")

    barrier = pltpu.get_barrier_semaphore()
    for axis, me, count in (("batch", my_group, groups), ("ctx", my_ctx, ctxs), ("head", my_head, heads)):
        for offset in range(1, count):
            pl.semaphore_signal(barrier, inc=1, device_id={axis: lax.rem(me + offset, count)}, device_id_type=MESH)

    slots = []
    for dst in range(groups):
        picked = [jnp.int32(0)] * capacity
        seen = jnp.int32(0)
        for j in range(per_owner):
            hit = shard_ref[dst, j] == my_group
            slot = slot_ref[dst, j]
            for k in range(capacity):
                picked[k] = jnp.where(hit & (seen == k), slot, picked[k])
            seen = seen + jnp.where(hit, 1, 0)
        slots.append(picked)

    sources = [shard_ref[my_group, j] for j in range(per_owner)]
    ranks, sides = [], []
    for j in range(per_owner):
        rank = jnp.int32(0)
        for i in range(j):
            rank = rank + jnp.where(sources[i] == sources[j], 1, 0)
        ranks.append(jnp.minimum(rank, capacity - 1))
        sides.append(jnp.where(sources[j] == sources[0], 0, 1))

    def split_kind(kind):
        width = 4 * rows
        row = lax.broadcasted_iota(jnp.int32, (rows, width), 0)
        col = lax.broadcasted_iota(jnp.int32, (rows, width), 1)
        pick = jnp.where(col == row * 4 + kind, 1.0, 0.0).astype(jnp.bfloat16)

        def one(dst, k):
            block = ingest_ref[slots[dst][k]]
            return jnp.dot(pick, block, preferred_element_type=jnp.float32).astype(jnp.bfloat16)

        return one

    masks = list(range(groups - 1, 0, -1))
    peers = {m: partner(my_group, m, groups) for m in masks}

    def fill(kind):
        one = split_kind(kind)
        for dst in range(groups):
            for k in range(capacity):
                if kind == UPDATE:
                    send_u[k, dst] = one(dst, k)
                else:
                    send_bufs[FIRST_KINDS.index(kind), dst, k] = one(dst, k)

    copies = {}

    def send(kind):
        if kind == UPDATE:
            for k in range(capacity):
                for m in masks:
                    copies[kind, k, m] = pltpu.make_async_remote_copy(
                        src_ref=send_u.at[k, peers[m]], dst_ref=recv_u[k].at[my_group],
                        send_sem=u_send.at[k, m], recv_sem=u_recv.at[k, m],
                        device_id={"batch": peers[m]}, device_id_type=MESH)
                    copies[kind, k, m].start()
                recv_u[k][my_group] = send_u[k, my_group]
            return
        n = FIRST_KINDS.index(kind)
        for m in masks:
            copies[kind, m] = pltpu.make_async_remote_copy(
                src_ref=send_bufs.at[n, peers[m]], dst_ref=recv_bufs[n].at[my_group],
                send_sem=z_send.at[n, m], recv_sem=z_recv.at[n, m],
                device_id={"batch": peers[m]}, device_id_type=MESH)
            copies[kind, m].start()
        recv_bufs[n][my_group] = send_bufs[n, my_group]

    def collect(kind, own_ref):
        n = FIRST_KINDS.index(kind)
        for m in masks:
            copies[kind, m].wait()
        for j in range(per_owner):
            own_ref[j * rows:(j + 1) * rows, :] = recv_bufs[n][sources[j], ranks[j]]

    fill(KEY)
    pl.semaphore_wait(barrier, groups + ctxs + heads - 3)
    send(KEY)
    fill(VALUE)
    send(VALUE)
    fill(QUERY)
    send(QUERY)
    fill(UPDATE)
    send(UPDATE)

    w_copies = []
    for offset in range(1, heads):
        to = lax.rem(my_head + offset, heads)
        copy = pltpu.make_async_remote_copy(
            src_ref=w_ref.at[:, pl.ds(pl.multiple_of(to * HD, HD), HD)], dst_ref=w_cols.at[my_head],
            send_sem=w_send.at[offset], recv_sem=w_recv.at[offset],
            device_id={"head": to}, device_id_type=MESH)
        copy.start()
        w_copies.append(copy)
    w_cols[my_head] = w_ref[:, pl.ds(pl.multiple_of(my_head * HD, HD), HD)]

    ends, total = [], jnp.int32(0)
    for u in range(hist_ref.shape[0]):
        total = total + hist_ref[u]
        ends.append(total)
    base = my_ctx * row_count
    position = base + lax.broadcasted_iota(jnp.int32, (row_count, HD), 0)
    first = jnp.zeros((row_count, HD), jnp.int32)
    for end in ends:
        first = jnp.where(position >= end, end, first)
    start_ref[...] = first - base

    def ctx_copy(n, own_ref, prev_ref, offset):
        return pltpu.make_async_remote_copy(
            src_ref=own_ref, dst_ref=prev_ref.at[offset - 1],
            send_sem=c_send.at[n, offset - 1], recv_sem=c_recv.at[n, offset - 1],
            device_id={"ctx": lax.rem(my_ctx + offset, ctxs)}, device_id_type=MESH)

    def push(n, own_ref, prev_ref):
        for offset in range(1, window + 1):
            @pl.when(my_ctx + offset < ctxs)
            def _():
                ctx_copy(n, own_ref, prev_ref, offset).start()

    collect(KEY, own_k)
    push(0, own_k, prev_k)
    collect(VALUE, own_v)
    push(1, own_v, prev_v)
    collect(QUERY, own_q)

    tile = 2 * rows if per_owner % 2 == 0 else rows
    tiles = row_count // tile
    half_scale = 0.5 / math.sqrt(HD)

    def attend(q, key_tile, value_tile, q_lo, k_lo, shift, causal):
        scores = lax.dot_general(q, key_tile, (((1,), (1,)), ((), ())), preferred_element_type=jnp.float32)
        half = scores * half_scale
        act = half + half * jnp.tanh(half)
        key_pos = lax.broadcasted_iota(jnp.int32, (tile, tile), 1) + (k_lo - shift)
        first_pos = jnp.concatenate([start_ref[q_lo:q_lo + tile, :]] * (tile // HD), axis=1)
        visible = key_pos >= first_pos
        if causal:
            visible = visible & (key_pos <= lax.broadcasted_iota(jnp.int32, (tile, tile), 0) + q_lo)
        weights = jnp.where(visible, act, 0.0).astype(jnp.bfloat16)
        return jnp.dot(weights, value_tile, preferred_element_type=jnp.float32)

    def put(i, value, add):
        for part in range(tile // rows):
            at = i * (tile // rows) + part
            piece = value[part * rows:(part + 1) * rows]
            att[at] = att[at] + piece if add else piece

    for i in range(tiles):
        q = own_q[i * tile:(i + 1) * tile, :]
        acc = None
        for t in range(i + 1):
            span = slice(t * tile, (t + 1) * tile)
            term = attend(q, own_k[span, :], own_v[span, :], i * tile, t * tile, 0, t == i)
            acc = term if acc is None else acc + term
        put(i, acc, False)
    for offset in range(1, window + 1):
        @pl.when(my_ctx >= offset)
        def _():
            ctx_copy(0, own_k, prev_k, offset).wait_recv()
            ctx_copy(1, own_v, prev_v, offset).wait_recv()
            for i in range(tiles):
                q = own_q[i * tile:(i + 1) * tile, :]
                acc = None
                for t in range(i if offset == window else 0, tiles):
                    span = slice(t * tile, (t + 1) * tile)
                    term = attend(q, prev_k[offset - 1, span, :], prev_v[offset - 1, span, :],
                                  i * tile, t * tile, offset * row_count, False)
                    acc = term if acc is None else acc + term
                put(i, acc, True)

    source_other = sources[0]
    for j in range(1, per_owner):
        source_other = jnp.where(sides[j] == 1, sources[j], source_other)
    side_source = (sources[0], source_other)
    h_copies = []
    for k in range(capacity):
        for m in masks:
            copies[UPDATE, k, m].wait()
        for side in range(2):
            at = jnp.int32(0)
            for j in range(per_owner):
                at = jnp.where((ranks[j] == k) & (sides[j] == side), j, at)
            rows_f32 = att[at]
            mean_square = jnp.mean(rows_f32 * rows_f32, axis=-1, keepdims=True)
            normed = rows_f32 * lax.rsqrt(mean_square + 1e-06)
            update = recv_u[k][side_source[side]].astype(jnp.float32)
            gated[k, my_head, side * rows:(side + 1) * rows, :] = (normed * update).astype(jnp.bfloat16)
        for offset in range(1, heads):
            copy = pltpu.make_async_remote_copy(
                src_ref=gated.at[k, my_head], dst_ref=gated.at[k, my_head],
                send_sem=h_send.at[k, offset], recv_sem=h_recv.at[k, offset],
                device_id={"head": lax.rem(my_head + offset, heads)}, device_id_type=MESH)
            copy.start()
            h_copies.append(copy)
    for copy in w_copies:
        copy.wait()
    for k in range(capacity):
        for copy in h_copies[k * (heads - 1):(k + 1) * (heads - 1)]:
            copy.wait()
        acc = None
        for h in range(heads):
            term = jnp.dot(gated[k, h], w_cols[h], preferred_element_type=jnp.float32)
            acc = term if acc is None else acc + term
        acc = acc.astype(jnp.bfloat16)
        for side in range(2):
            mixed[2 * k + side] = acc[side * rows:(side + 1) * rows]
    for j in range(per_owner):
        out_ref[j * rows:(j + 1) * rows, :] = mixed[2 * ranks[j] + sides[j]]
    for offset in range(1, window + 1):
        @pl.when(my_ctx + offset < ctxs)
        def _():
            ctx_copy(0, own_k, prev_k, offset).wait_send()
            ctx_copy(1, own_v, prev_v, offset).wait_send()


def body(ingest, src_shard, src_slot, hist_len, w_out):
    groups, ctxs, heads = (lax.axis_size(a) for a in ("batch", "ctx", "head"))
    slot_total, rows, kinds, width = ingest.shape[2:]
    per_owner = src_shard.shape[2]
    capacity = per_owner // 2
    window = ctxs // 2
    row_count = per_owner * rows
    bf16 = jnp.bfloat16
    dma = pltpu.SemaphoreType.DMA
    vmem = pl.BlockSpec(memory_space=pltpu.VMEM)
    smem = pl.BlockSpec(memory_space=pltpu.SMEM)
    mixed = pl.pallas_call(
        functools.partial(kernel, (groups, ctxs, heads, per_owner, rows)),
        out_shape=jax.ShapeDtypeStruct((row_count, width), bf16),
        in_specs=[smem, smem, smem, vmem, vmem],
        out_specs=vmem,
        scratch_shapes=[
            pltpu.VMEM((3, groups, capacity, rows, width), bf16),
            pltpu.VMEM((capacity, groups, rows, width), bf16),
            [pltpu.VMEM((groups, capacity, rows, width), bf16)] * 3,
            [pltpu.VMEM((groups, rows, width), bf16)] * capacity,
            pltpu.VMEM((row_count, width), bf16),
            pltpu.VMEM((row_count, width), bf16),
            pltpu.VMEM((row_count, width), bf16),
            pltpu.VMEM((window, row_count, width), bf16),
            pltpu.VMEM((window, row_count, width), bf16),
            pltpu.VMEM((row_count, width), jnp.int32),
            pltpu.VMEM((per_owner, rows, width), jnp.float32),
            pltpu.VMEM((capacity, heads, 2 * rows, width), bf16),
            pltpu.VMEM((heads, width, width), bf16),
            pltpu.VMEM((per_owner, rows, width), bf16),
            dma((3, groups)), dma((3, groups)),
            dma((capacity, groups)), dma((capacity, groups)),
            dma((2, window)), dma((2, window)),
            dma((capacity, heads)), dma((capacity, heads)),
            dma((heads,)), dma((heads,)),
        ],
        compiler_params=pltpu.CompilerParams(
            collective_id=0, has_side_effects=True, vmem_limit_bytes=56 * 1024 * 1024),
    )(src_shard[0], src_slot[0], hist_len[0],
      ingest.reshape(slot_total, rows * kinds, width), w_out)
    return mixed[None]


def solution(mesh):
    in_specs = (
        P("ctx", "batch", None, None, None, "head"),
        P("ctx", None, None),
        P("ctx", None, None),
        P("batch", None),
        P("head", None),
    )
    out_specs = P("batch", "ctx", "head")
    return jax.shard_map(body, mesh=mesh, in_specs=in_specs, out_specs=out_specs, check_vma=False)
```

```python
import functools
import math

import jax
import jax.numpy as jnp
from jax import lax
from jax.experimental import pallas as pl
from jax.experimental.pallas import tpu as pltpu
from jax.sharding import PartitionSpec as P

HD = 128
MESH = pl.DeviceIdType.MESH
QUERY, KEY, VALUE, UPDATE = 0, 1, 2, 3
FIRST_KINDS = (KEY, VALUE, QUERY)


def partner(me, mask, count):
    out = 0
    bit = 1
    while bit < count:
        out = out + lax.rem(lax.div(me, bit) + (mask // bit) % 2, 2) * bit
        bit *= 2
    return out


def update_chunks(capacity, rows):
    half = rows // 2
    return [(k, 0, rows) for k in range(capacity - 1)] + [(capacity - 1, 0, half), (capacity - 1, half, half)]


def kernel(sizes, shard_ref, slot_ref, hist_ref, ingest_hbm, w_ref, out_ref,
           ingest_ref,
           send_bufs, send_u, recv_bufs, recv_u, own_k, own_v, own_q, prev_k, prev_v,
           start_ref, att, gated, w_cols, mixed,
           z_send, z_recv, u_send, u_recv, c_send, c_recv, h_send, h_recv, w_send, w_recv,
           ingest_sem, from_low, from_high):
    groups, ctxs, heads, per_owner, rows = sizes
    capacity = per_owner // 2
    chunks = update_chunks(capacity, rows)
    window = ctxs // 2
    row_count = per_owner * rows
    my_group = lax.axis_index("batch")
    my_ctx = lax.axis_index("ctx")
    my_head = lax.axis_index("head")

    barrier = pltpu.get_barrier_semaphore()
    ingest_copy = pltpu.make_async_copy(ingest_hbm, ingest_ref, ingest_sem)
    ingest_copy.start()
    for axis, me, count in (("ctx", my_ctx, ctxs), ("head", my_head, heads)):
        for offset in range(1, count):
            pl.semaphore_signal(barrier, inc=1, device_id={axis: lax.rem(me + offset, count)}, device_id_type=MESH)
    has_low, has_high = my_group > 0, my_group < groups - 1

    def tell(there, semaphore, to):
        @pl.when(there)
        def _():
            pl.semaphore_signal(semaphore, inc=1, device_id={"batch": to}, device_id_type=MESH)

    tell(has_low, barrier, my_group - 1)
    tell(has_high, barrier, my_group + 1)
    neighbours = jnp.where(has_low, 1, 0) + jnp.where(has_high, 1, 0)

    slots = []
    for dst in range(groups):
        picked = [jnp.int32(0)] * capacity
        seen = jnp.int32(0)
        for j in range(per_owner):
            hit = shard_ref[dst, j] == my_group
            slot = slot_ref[dst, j]
            for k in range(capacity):
                picked[k] = jnp.where(hit & (seen == k), slot, picked[k])
            seen = seen + jnp.where(hit, 1, 0)
        slots.append(picked)

    sources = [shard_ref[my_group, j] for j in range(per_owner)]
    ranks, sides = [], []
    for j in range(per_owner):
        rank = jnp.int32(0)
        for i in range(j):
            rank = rank + jnp.where(sources[i] == sources[j], 1, 0)
        ranks.append(jnp.minimum(rank, capacity - 1))
        sides.append(jnp.where(sources[j] == sources[0], 0, 1))

    def split_kind(kind):
        width = 4 * rows
        row = lax.broadcasted_iota(jnp.int32, (rows, width), 0)
        col = lax.broadcasted_iota(jnp.int32, (rows, width), 1)
        pick = jnp.where(col == row * 4 + kind, 1.0, 0.0).astype(jnp.bfloat16)

        def one(dst, k):
            block = ingest_ref[slots[dst][k]]
            return jnp.dot(pick, block, preferred_element_type=jnp.float32).astype(jnp.bfloat16)

        return one

    masks = list(range(groups - 1, 0, -1))
    peers = {m: partner(my_group, m, groups) for m in masks}

    def fill(kind):
        one = split_kind(kind)
        for dst in range(groups):
            for k in range(capacity):
                if kind == UPDATE:
                    block = one(dst, k)
                    for c, (of, low, size) in enumerate(chunks):
                        if of == k:
                            send_u[c][dst] = block[low:low + size]
                else:
                    send_bufs[FIRST_KINDS.index(kind), dst, k] = one(dst, k)

    copies = {}

    def send(kind):
        if kind == UPDATE:
            for c in range(len(chunks)):
                for m in masks:
                    copies[kind, c, m] = pltpu.make_async_remote_copy(
                        src_ref=send_u[c].at[peers[m]], dst_ref=recv_u[c].at[my_group],
                        send_sem=u_send.at[c, m], recv_sem=u_recv.at[c, m],
                        device_id={"batch": peers[m]}, device_id_type=MESH)
                    copies[kind, c, m].start()
                recv_u[c][my_group] = send_u[c][my_group]
            return
        n = FIRST_KINDS.index(kind)
        for m in masks:
            copies[kind, m] = pltpu.make_async_remote_copy(
                src_ref=send_bufs.at[n, peers[m]], dst_ref=recv_bufs[n].at[my_group],
                send_sem=z_send.at[n, m], recv_sem=z_recv.at[n, m],
                device_id={"batch": peers[m]}, device_id_type=MESH)
            if kind != KEY:
                copies[kind, m].start()
        recv_bufs[n][my_group] = send_bufs[n, my_group]

    def collect(kind, own_ref):
        n = FIRST_KINDS.index(kind)
        for m in masks:
            copies[kind, m].wait()
        for j in range(per_owner):
            own_ref[j * rows:(j + 1) * rows, :] = recv_bufs[n][sources[j], ranks[j]]

    def start_at(distance):
        for m in masks:
            @pl.when((peers[m] - my_group == distance) | (my_group - peers[m] == distance))
            def _():
                copies[KEY, m].start()

    def hear(distance):
        for there, semaphore in ((my_group >= distance, from_low), (my_group + distance < groups, from_high)):
            @pl.when(there)
            def _():
                pl.semaphore_wait(semaphore.at[distance], 1)

    def pass_on(distance):
        tell((my_group >= distance) & has_high, from_low.at[distance + 1], my_group + 1)
        tell((my_group + distance < groups) & has_low, from_high.at[distance + 1], my_group - 1)

    ingest_copy.wait()
    fill(KEY)
    pl.semaphore_wait(barrier, neighbours + ctxs + heads - 2)
    if groups > 2:
        pass_on(1)
    send(KEY)
    start_at(1)
    fill(VALUE)
    for distance in range(2, groups):
        hear(distance)
        if distance + 1 < groups:
            pass_on(distance)
        start_at(distance)
    send(VALUE)
    fill(QUERY)
    send(QUERY)
    fill(UPDATE)
    send(UPDATE)

    w_copies = []
    for offset in range(1, heads):
        to = lax.rem(my_head + offset, heads)
        copy = pltpu.make_async_remote_copy(
            src_ref=w_ref.at[:, pl.ds(pl.multiple_of(to * HD, HD), HD)], dst_ref=w_cols.at[my_head],
            send_sem=w_send.at[offset], recv_sem=w_recv.at[offset],
            device_id={"head": to}, device_id_type=MESH)
        copy.start()
        w_copies.append(copy)
    w_cols[my_head] = w_ref[:, pl.ds(pl.multiple_of(my_head * HD, HD), HD)]

    ends, total = [], jnp.int32(0)
    for u in range(hist_ref.shape[0]):
        total = total + hist_ref[u]
        ends.append(total)
    base = my_ctx * row_count
    position = base + lax.broadcasted_iota(jnp.int32, (row_count, HD), 0)
    first = jnp.zeros((row_count, HD), jnp.int32)
    for end in ends:
        first = jnp.where(position >= end, end, first)
    start_ref[...] = first - base

    def ctx_copy(n, own_ref, prev_ref, offset):
        return pltpu.make_async_remote_copy(
            src_ref=own_ref, dst_ref=prev_ref.at[offset - 1],
            send_sem=c_send.at[n, offset - 1], recv_sem=c_recv.at[n, offset - 1],
            device_id={"ctx": lax.rem(my_ctx + offset, ctxs)}, device_id_type=MESH)

    def push(n, own_ref, prev_ref):
        for offset in range(1, window + 1):
            @pl.when(my_ctx + offset < ctxs)
            def _():
                ctx_copy(n, own_ref, prev_ref, offset).start()

    collect(KEY, own_k)
    push(0, own_k, prev_k)
    collect(VALUE, own_v)
    push(1, own_v, prev_v)
    collect(QUERY, own_q)

    tile = 2 * rows if per_owner % 2 == 0 else rows
    tiles = row_count // tile
    half_scale = 0.5 / math.sqrt(HD)

    def attend(q, key_tile, value_tile, q_lo, k_lo, shift, causal):
        scores = lax.dot_general(q, key_tile, (((1,), (1,)), ((), ())), preferred_element_type=jnp.float32)
        half = scores * half_scale
        act = half + half * jnp.tanh(half)
        key_pos = lax.broadcasted_iota(jnp.int32, (tile, tile), 1) + (k_lo - shift)
        first_pos = jnp.concatenate([start_ref[q_lo:q_lo + tile, :]] * (tile // HD), axis=1)
        visible = key_pos >= first_pos
        if causal:
            visible = visible & (key_pos <= lax.broadcasted_iota(jnp.int32, (tile, tile), 0) + q_lo)
        weights = jnp.where(visible, act, 0.0).astype(jnp.bfloat16)
        return jnp.dot(weights, value_tile, preferred_element_type=jnp.float32)

    def put(i, value, add):
        for part in range(tile // rows):
            at = i * (tile // rows) + part
            piece = value[part * rows:(part + 1) * rows]
            att[at] = att[at] + piece if add else piece

    for i in range(tiles):
        q = own_q[i * tile:(i + 1) * tile, :]
        acc = None
        for t in range(i + 1):
            span = slice(t * tile, (t + 1) * tile)
            term = attend(q, own_k[span, :], own_v[span, :], i * tile, t * tile, 0, t == i)
            acc = term if acc is None else acc + term
        put(i, acc, False)
    for offset in range(1, window + 1):
        @pl.when(my_ctx >= offset)
        def _():
            ctx_copy(0, own_k, prev_k, offset).wait_recv()
            ctx_copy(1, own_v, prev_v, offset).wait_recv()
            for i in range(tiles):
                q = own_q[i * tile:(i + 1) * tile, :]
                acc = None
                for t in range(i if offset == window else 0, tiles):
                    span = slice(t * tile, (t + 1) * tile)
                    term = attend(q, prev_k[offset - 1, span, :], prev_v[offset - 1, span, :],
                                  i * tile, t * tile, offset * row_count, False)
                    acc = term if acc is None else acc + term
                put(i, acc, True)

    source_other = sources[0]
    for j in range(1, per_owner):
        source_other = jnp.where(sides[j] == 1, sources[j], source_other)
    side_source = (sources[0], source_other)
    h_copies = []
    for c, (k, low, size) in enumerate(chunks):
        for m in masks:
            copies[UPDATE, c, m].wait()
        for side in range(2):
            at = jnp.int32(0)
            for j in range(per_owner):
                at = jnp.where((ranks[j] == k) & (sides[j] == side), j, at)
            rows_f32 = att[at, low:low + size, :]
            mean_square = jnp.mean(rows_f32 * rows_f32, axis=-1, keepdims=True)
            normed = rows_f32 * lax.rsqrt(mean_square + 1e-06)
            update = recv_u[c][side_source[side]].astype(jnp.float32)
            gated[c][my_head, side * size:(side + 1) * size, :] = (normed * update).astype(jnp.bfloat16)
        for offset in range(1, heads):
            copy = pltpu.make_async_remote_copy(
                src_ref=gated[c].at[my_head], dst_ref=gated[c].at[my_head],
                send_sem=h_send.at[c, offset], recv_sem=h_recv.at[c, offset],
                device_id={"head": lax.rem(my_head + offset, heads)}, device_id_type=MESH)
            copy.start()
            h_copies.append(copy)
    for copy in w_copies:
        copy.wait()
    for c, (k, low, size) in enumerate(chunks):
        for copy in h_copies[c * (heads - 1):(c + 1) * (heads - 1)]:
            copy.wait()
        acc = None
        for h in range(heads):
            term = jnp.dot(gated[c][h], w_cols[h], preferred_element_type=jnp.float32)
            acc = term if acc is None else acc + term
        acc = acc.astype(jnp.bfloat16)
        for side in range(2):
            mixed[2 * k + side, low:low + size, :] = acc[side * size:(side + 1) * size]
    for j in range(per_owner):
        out_ref[j * rows:(j + 1) * rows, :] = mixed[2 * ranks[j] + sides[j]]
    for offset in range(1, window + 1):
        @pl.when(my_ctx + offset < ctxs)
        def _():
            ctx_copy(0, own_k, prev_k, offset).wait_send()
            ctx_copy(1, own_v, prev_v, offset).wait_send()


def body(ingest, src_shard, src_slot, hist_len, w_out):
    groups, ctxs, heads = (lax.axis_size(a) for a in ("batch", "ctx", "head"))
    slot_total, rows, kinds, width = ingest.shape[2:]
    per_owner = src_shard.shape[2]
    capacity = per_owner // 2
    chunks = update_chunks(capacity, rows)
    window = ctxs // 2
    row_count = per_owner * rows
    bf16 = jnp.bfloat16
    dma = pltpu.SemaphoreType.DMA
    vmem = pl.BlockSpec(memory_space=pltpu.VMEM)
    smem = pl.BlockSpec(memory_space=pltpu.SMEM)
    mixed = pl.pallas_call(
        functools.partial(kernel, (groups, ctxs, heads, per_owner, rows)),
        out_shape=jax.ShapeDtypeStruct((row_count, width), bf16),
        in_specs=[smem, smem, smem, pl.BlockSpec(memory_space=pl.ANY), vmem],
        out_specs=vmem,
        scratch_shapes=[
            pltpu.VMEM((slot_total, rows * kinds, width), bf16),
            pltpu.VMEM((3, groups, capacity, rows, width), bf16),
            [pltpu.VMEM((groups, size, width), bf16) for _, _, size in chunks],
            [pltpu.VMEM((groups, capacity, rows, width), bf16)] * 3,
            [pltpu.VMEM((groups, size, width), bf16) for _, _, size in chunks],
            pltpu.VMEM((row_count, width), bf16),
            pltpu.VMEM((row_count, width), bf16),
            pltpu.VMEM((row_count, width), bf16),
            pltpu.VMEM((window, row_count, width), bf16),
            pltpu.VMEM((window, row_count, width), bf16),
            pltpu.VMEM((row_count, width), jnp.int32),
            pltpu.VMEM((per_owner, rows, width), jnp.float32),
            [pltpu.VMEM((heads, 2 * size, width), bf16) for _, _, size in chunks],
            pltpu.VMEM((heads, width, width), bf16),
            pltpu.VMEM((per_owner, rows, width), bf16),
            dma((3, groups)), dma((3, groups)),
            dma((len(chunks), groups)), dma((len(chunks), groups)),
            dma((2, window)), dma((2, window)),
            dma((len(chunks), heads)), dma((len(chunks), heads)),
            dma((heads,)), dma((heads,)),
            dma, pltpu.SemaphoreType.REGULAR((groups,)), pltpu.SemaphoreType.REGULAR((groups,)),
        ],
        compiler_params=pltpu.CompilerParams(
            collective_id=0, has_side_effects=True, vmem_limit_bytes=56 * 1024 * 1024),
    )(src_shard[0], src_slot[0], hist_len[0],
      ingest.reshape(slot_total, rows * kinds, width), w_out)
    return mixed[None]


def solution(mesh):
    in_specs = (
        P("ctx", "batch", None, None, None, "head"),
        P("ctx", None, None),
        P("ctx", None, None),
        P("batch", None),
        P("head", None),
    )
    out_specs = P("batch", "ctx", "head")
    return jax.shard_map(body, mesh=mesh, in_specs=in_specs, out_specs=out_specs, check_vma=False)
```

```python
import functools
import math

import jax
import jax.numpy as jnp
from jax import lax
from jax.experimental import pallas as pl
from jax.experimental.pallas import tpu as pltpu
from jax.sharding import PartitionSpec as P

HD = 128
MESH = pl.DeviceIdType.MESH
QUERY, KEY, VALUE, UPDATE = 0, 1, 2, 3
FIRST_KINDS = (KEY, VALUE, QUERY)


def partner(me, mask, count):
    out = 0
    bit = 1
    while bit < count:
        out = out + lax.rem(lax.div(me, bit) + (mask // bit) % 2, 2) * bit
        bit *= 2
    return out


def update_chunks(capacity, rows):
    half = rows // 2
    return [(k, 0, rows) for k in range(capacity - 1)] + [(capacity - 1, 0, half), (capacity - 1, half, half)]


def kernel(sizes, shard_hbm, slot_hbm, hist_hbm, ingest_hbm, w_hbm, out_ref,
           shard_ref, slot_ref, hist_ref, w_ref, local_sems,
           ingest_ref,
           send_bufs, send_u, recv_bufs, recv_u, own_k, own_v, own_q, prev_k, prev_v,
           start_ref, att, gated, w_cols, mixed,
           z_send, z_recv, u_send, u_recv, c_send, c_recv, h_send, h_recv, w_send, w_recv,
           ingest_sem, from_low, from_high):
    groups, ctxs, heads, per_owner, rows = sizes
    capacity = per_owner // 2
    chunks = update_chunks(capacity, rows)
    window = ctxs // 2
    row_count = per_owner * rows
    my_group = lax.axis_index("batch")
    my_ctx = lax.axis_index("ctx")
    my_head = lax.axis_index("head")

    barrier = pltpu.get_barrier_semaphore()
    ingest_copy = pltpu.make_async_copy(ingest_hbm, ingest_ref, ingest_sem)
    ingest_copy.start()
    local_copies = [pltpu.make_async_copy(src, dst, local_sems.at[i]) for i, (src, dst) in enumerate((
        (shard_hbm, shard_ref), (slot_hbm, slot_ref), (hist_hbm, hist_ref), (w_hbm, w_ref)))]
    for copy in local_copies:
        copy.start()
    for axis, me, count in (("ctx", my_ctx, ctxs), ("head", my_head, heads)):
        for offset in range(1, count):
            pl.semaphore_signal(barrier, inc=1, device_id={axis: lax.rem(me + offset, count)}, device_id_type=MESH)
    has_low, has_high = my_group > 0, my_group < groups - 1

    def tell(there, semaphore, to):
        @pl.when(there)
        def _():
            pl.semaphore_signal(semaphore, inc=1, device_id={"batch": to}, device_id_type=MESH)

    tell(has_low, barrier, my_group - 1)
    tell(has_high, barrier, my_group + 1)
    neighbours = jnp.where(has_low, 1, 0) + jnp.where(has_high, 1, 0)

    for copy in local_copies:
        copy.wait()
    slots = []
    for dst in range(groups):
        picked = [jnp.int32(0)] * capacity
        seen = jnp.int32(0)
        for j in range(per_owner):
            hit = shard_ref[dst, j] == my_group
            slot = slot_ref[dst, j]
            for k in range(capacity):
                picked[k] = jnp.where(hit & (seen == k), slot, picked[k])
            seen = seen + jnp.where(hit, 1, 0)
        slots.append(picked)

    sources = [shard_ref[my_group, j] for j in range(per_owner)]
    ranks, sides = [], []
    for j in range(per_owner):
        rank = jnp.int32(0)
        for i in range(j):
            rank = rank + jnp.where(sources[i] == sources[j], 1, 0)
        ranks.append(jnp.minimum(rank, capacity - 1))
        sides.append(jnp.where(sources[j] == sources[0], 0, 1))

    def split_kind(kind):
        width = 4 * rows
        row = lax.broadcasted_iota(jnp.int32, (rows, width), 0)
        col = lax.broadcasted_iota(jnp.int32, (rows, width), 1)
        pick = jnp.where(col == row * 4 + kind, 1.0, 0.0).astype(jnp.bfloat16)

        def one(dst, k):
            block = ingest_ref[slots[dst][k]]
            return jnp.dot(pick, block, preferred_element_type=jnp.float32).astype(jnp.bfloat16)

        return one

    masks = list(range(groups - 1, 0, -1))
    peers = {m: partner(my_group, m, groups) for m in masks}

    def fill(kind):
        one = split_kind(kind)
        for dst in range(groups):
            for k in range(capacity):
                if kind == UPDATE:
                    block = one(dst, k)
                    for c, (of, low, size) in enumerate(chunks):
                        if of == k:
                            send_u[c][dst] = block[low:low + size]
                else:
                    send_bufs[FIRST_KINDS.index(kind), dst, k] = one(dst, k)

    copies = {}

    def send(kind):
        if kind == UPDATE:
            for c in range(len(chunks)):
                for m in masks:
                    copies[kind, c, m] = pltpu.make_async_remote_copy(
                        src_ref=send_u[c].at[peers[m]], dst_ref=recv_u[c].at[my_group],
                        send_sem=u_send.at[c, m], recv_sem=u_recv.at[c, m],
                        device_id={"batch": peers[m]}, device_id_type=MESH)
                    copies[kind, c, m].start()
                recv_u[c][my_group] = send_u[c][my_group]
            return
        n = FIRST_KINDS.index(kind)
        for m in masks:
            copies[kind, m] = pltpu.make_async_remote_copy(
                src_ref=send_bufs.at[n, peers[m]], dst_ref=recv_bufs[n].at[my_group],
                send_sem=z_send.at[n, m], recv_sem=z_recv.at[n, m],
                device_id={"batch": peers[m]}, device_id_type=MESH)
            if kind != KEY:
                copies[kind, m].start()
        recv_bufs[n][my_group] = send_bufs[n, my_group]

    def collect(kind, own_ref):
        n = FIRST_KINDS.index(kind)
        for m in masks:
            copies[kind, m].wait()
        for j in range(per_owner):
            own_ref[j * rows:(j + 1) * rows, :] = recv_bufs[n][sources[j], ranks[j]]

    def start_at(distance):
        for m in masks:
            @pl.when((peers[m] - my_group == distance) | (my_group - peers[m] == distance))
            def _():
                copies[KEY, m].start()

    def hear(distance):
        for there, semaphore in ((my_group >= distance, from_low), (my_group + distance < groups, from_high)):
            @pl.when(there)
            def _():
                pl.semaphore_wait(semaphore.at[distance], 1)

    def pass_on(distance):
        tell((my_group >= distance) & has_high, from_low.at[distance + 1], my_group + 1)
        tell((my_group + distance < groups) & has_low, from_high.at[distance + 1], my_group - 1)

    ingest_copy.wait()
    fill(KEY)
    pl.semaphore_wait(barrier, neighbours + ctxs + heads - 2)
    if groups > 2:
        pass_on(1)
    send(KEY)
    start_at(1)
    fill(VALUE)
    for distance in range(2, groups):
        hear(distance)
        if distance + 1 < groups:
            pass_on(distance)
        start_at(distance)
    send(VALUE)
    fill(QUERY)
    send(QUERY)
    fill(UPDATE)
    send(UPDATE)

    w_copies = []
    for offset in range(1, heads):
        to = lax.rem(my_head + offset, heads)
        copy = pltpu.make_async_remote_copy(
            src_ref=w_ref.at[:, pl.ds(pl.multiple_of(to * HD, HD), HD)], dst_ref=w_cols.at[my_head],
            send_sem=w_send.at[offset], recv_sem=w_recv.at[offset],
            device_id={"head": to}, device_id_type=MESH)
        copy.start()
        w_copies.append(copy)
    w_cols[my_head] = w_ref[:, pl.ds(pl.multiple_of(my_head * HD, HD), HD)]

    ends, total = [], jnp.int32(0)
    for u in range(hist_ref.shape[0]):
        total = total + hist_ref[u]
        ends.append(total)
    base = my_ctx * row_count
    position = base + lax.broadcasted_iota(jnp.int32, (row_count, HD), 0)
    first = jnp.zeros((row_count, HD), jnp.int32)
    for end in ends:
        first = jnp.where(position >= end, end, first)
    start_ref[...] = first - base

    def ctx_copy(n, own_ref, prev_ref, offset):
        return pltpu.make_async_remote_copy(
            src_ref=own_ref, dst_ref=prev_ref.at[offset - 1],
            send_sem=c_send.at[n, offset - 1], recv_sem=c_recv.at[n, offset - 1],
            device_id={"ctx": lax.rem(my_ctx + offset, ctxs)}, device_id_type=MESH)

    def push(n, own_ref, prev_ref):
        for offset in range(1, window + 1):
            @pl.when(my_ctx + offset < ctxs)
            def _():
                ctx_copy(n, own_ref, prev_ref, offset).start()

    collect(KEY, own_k)
    push(0, own_k, prev_k)
    collect(VALUE, own_v)
    push(1, own_v, prev_v)
    collect(QUERY, own_q)

    tile = 2 * rows if per_owner % 2 == 0 else rows
    tiles = row_count // tile
    half_scale = 0.5 / math.sqrt(HD)

    def attend(q, key_tile, value_tile, q_lo, k_lo, shift, causal):
        scores = lax.dot_general(q, key_tile, (((1,), (1,)), ((), ())), preferred_element_type=jnp.float32)
        half = scores * half_scale
        act = half + half * jnp.tanh(half)
        key_pos = lax.broadcasted_iota(jnp.int32, (tile, tile), 1) + (k_lo - shift)
        first_pos = jnp.concatenate([start_ref[q_lo:q_lo + tile, :]] * (tile // HD), axis=1)
        visible = key_pos >= first_pos
        if causal:
            visible = visible & (key_pos <= lax.broadcasted_iota(jnp.int32, (tile, tile), 0) + q_lo)
        weights = jnp.where(visible, act, 0.0).astype(jnp.bfloat16)
        return jnp.dot(weights, value_tile, preferred_element_type=jnp.float32)

    def put(i, value, add):
        for part in range(tile // rows):
            at = i * (tile // rows) + part
            piece = value[part * rows:(part + 1) * rows]
            att[at] = att[at] + piece if add else piece

    for i in range(tiles):
        q = own_q[i * tile:(i + 1) * tile, :]
        acc = None
        for t in range(i + 1):
            span = slice(t * tile, (t + 1) * tile)
            term = attend(q, own_k[span, :], own_v[span, :], i * tile, t * tile, 0, t == i)
            acc = term if acc is None else acc + term
        put(i, acc, False)
    for offset in range(1, window + 1):
        @pl.when(my_ctx >= offset)
        def _():
            ctx_copy(0, own_k, prev_k, offset).wait_recv()
            ctx_copy(1, own_v, prev_v, offset).wait_recv()
            for i in range(tiles):
                q = own_q[i * tile:(i + 1) * tile, :]
                acc = None
                for t in range(i if offset == window else 0, tiles):
                    span = slice(t * tile, (t + 1) * tile)
                    term = attend(q, prev_k[offset - 1, span, :], prev_v[offset - 1, span, :],
                                  i * tile, t * tile, offset * row_count, False)
                    acc = term if acc is None else acc + term
                put(i, acc, True)

    source_other = sources[0]
    for j in range(1, per_owner):
        source_other = jnp.where(sides[j] == 1, sources[j], source_other)
    side_source = (sources[0], source_other)
    h_copies = []
    for c, (k, low, size) in enumerate(chunks):
        for m in masks:
            copies[UPDATE, c, m].wait()
        for side in range(2):
            at = jnp.int32(0)
            for j in range(per_owner):
                at = jnp.where((ranks[j] == k) & (sides[j] == side), j, at)
            rows_f32 = att[at, low:low + size, :]
            mean_square = jnp.mean(rows_f32 * rows_f32, axis=-1, keepdims=True)
            normed = rows_f32 * lax.rsqrt(mean_square + 1e-06)
            update = recv_u[c][side_source[side]].astype(jnp.float32)
            gated[c][my_head, side * size:(side + 1) * size, :] = (normed * update).astype(jnp.bfloat16)
        for offset in range(1, heads):
            copy = pltpu.make_async_remote_copy(
                src_ref=gated[c].at[my_head], dst_ref=gated[c].at[my_head],
                send_sem=h_send.at[c, offset], recv_sem=h_recv.at[c, offset],
                device_id={"head": lax.rem(my_head + offset, heads)}, device_id_type=MESH)
            copy.start()
            h_copies.append(copy)
    for copy in w_copies:
        copy.wait()
    for c, (k, low, size) in enumerate(chunks):
        for copy in h_copies[c * (heads - 1):(c + 1) * (heads - 1)]:
            copy.wait()
        acc = None
        for h in range(heads):
            term = jnp.dot(gated[c][h], w_cols[h], preferred_element_type=jnp.float32)
            acc = term if acc is None else acc + term
        acc = acc.astype(jnp.bfloat16)
        for side in range(2):
            mixed[2 * k + side, low:low + size, :] = acc[side * size:(side + 1) * size]
    for j in range(per_owner):
        out_ref[j * rows:(j + 1) * rows, :] = mixed[2 * ranks[j] + sides[j]]
    for offset in range(1, window + 1):
        @pl.when(my_ctx + offset < ctxs)
        def _():
            ctx_copy(0, own_k, prev_k, offset).wait_send()
            ctx_copy(1, own_v, prev_v, offset).wait_send()


def body(ingest, src_shard, src_slot, hist_len, w_out):
    groups, ctxs, heads = (lax.axis_size(a) for a in ("batch", "ctx", "head"))
    slot_total, rows, kinds, width = ingest.shape[2:]
    per_owner = src_shard.shape[2]
    capacity = per_owner // 2
    chunks = update_chunks(capacity, rows)
    window = ctxs // 2
    row_count = per_owner * rows
    bf16 = jnp.bfloat16
    dma = pltpu.SemaphoreType.DMA
    vmem = pl.BlockSpec(memory_space=pltpu.VMEM)
    mixed = pl.pallas_call(
        functools.partial(kernel, (groups, ctxs, heads, per_owner, rows)),
        out_shape=jax.ShapeDtypeStruct((row_count, width), bf16),
        in_specs=[pl.BlockSpec(memory_space=pl.ANY)] * 5,
        out_specs=vmem,
        scratch_shapes=[
            pltpu.SMEM(src_shard.shape[1:], jnp.int32), pltpu.SMEM(src_slot.shape[1:], jnp.int32),
            pltpu.SMEM(hist_len.shape[1:], jnp.int32), pltpu.VMEM(w_out.shape, bf16), dma((4,)),
            pltpu.VMEM((slot_total, rows * kinds, width), bf16),
            pltpu.VMEM((3, groups, capacity, rows, width), bf16),
            [pltpu.VMEM((groups, size, width), bf16) for _, _, size in chunks],
            [pltpu.VMEM((groups, capacity, rows, width), bf16)] * 3,
            [pltpu.VMEM((groups, size, width), bf16) for _, _, size in chunks],
            pltpu.VMEM((row_count, width), bf16),
            pltpu.VMEM((row_count, width), bf16),
            pltpu.VMEM((row_count, width), bf16),
            pltpu.VMEM((window, row_count, width), bf16),
            pltpu.VMEM((window, row_count, width), bf16),
            pltpu.VMEM((row_count, width), jnp.int32),
            pltpu.VMEM((per_owner, rows, width), jnp.float32),
            [pltpu.VMEM((heads, 2 * size, width), bf16) for _, _, size in chunks],
            pltpu.VMEM((heads, width, width), bf16),
            pltpu.VMEM((per_owner, rows, width), bf16),
            dma((3, groups)), dma((3, groups)),
            dma((len(chunks), groups)), dma((len(chunks), groups)),
            dma((2, window)), dma((2, window)),
            dma((len(chunks), heads)), dma((len(chunks), heads)),
            dma((heads,)), dma((heads,)),
            dma, pltpu.SemaphoreType.REGULAR((groups,)), pltpu.SemaphoreType.REGULAR((groups,)),
        ],
        compiler_params=pltpu.CompilerParams(
            collective_id=0, has_side_effects=True, vmem_limit_bytes=56 * 1024 * 1024),
    )(src_shard[0], src_slot[0], hist_len[0],
      ingest.reshape(slot_total, rows * kinds, width), w_out)
    return mixed[None]


def solution(mesh):
    in_specs = (
        P("ctx", "batch", None, None, None, "head"),
        P("ctx", None, None),
        P("ctx", None, None),
        P("batch", None),
        P("head", None),
    )
    out_specs = P("batch", "ctx", "head")
    return jax.shard_map(body, mesh=mesh, in_specs=in_specs, out_specs=out_specs, check_vma=False)
```

```python
import functools
import math

import jax
import jax.numpy as jnp
from jax import lax
from jax.experimental import pallas as pl
from jax.experimental.pallas import tpu as pltpu
from jax.sharding import PartitionSpec as P

HD = 128
MESH = pl.DeviceIdType.MESH
QUERY, KEY, VALUE, UPDATE = 0, 1, 2, 3
FIRST_KINDS = (KEY, VALUE, QUERY)


def partner(me, mask, count):
    out = 0
    bit = 1
    while bit < count:
        out = out + lax.rem(lax.div(me, bit) + (mask // bit) % 2, 2) * bit
        bit *= 2
    return out


def update_chunks(capacity, rows):
    half = rows // 2
    return [(k, 0, rows) for k in range(capacity - 1)] + [(capacity - 1, 0, half), (capacity - 1, half, half)]


def kernel(sizes, shard_hbm, slot_hbm, hist_hbm, ingest_hbm, w_hbm, out_ref,
           shard_ref, slot_ref, hist_ref, w_ref, local_sems,
           ingest_ref,
           send_bufs, send_u, recv_bufs, recv_u, own_k, own_v, own_q, prev_k, prev_v,
           start_ref, att, gated, w_cols, mixed,
           z_send, z_recv, u_send, u_recv, c_send, c_recv, h_send, h_recv, w_send, w_recv,
           ingest_sem, from_low, from_high):
    groups, ctxs, heads, per_owner, rows = sizes
    capacity = per_owner // 2
    chunks = update_chunks(capacity, rows)
    window = ctxs // 2
    row_count = per_owner * rows
    my_group = lax.axis_index("batch")
    my_ctx = lax.axis_index("ctx")
    my_head = lax.axis_index("head")

    barrier = pltpu.get_barrier_semaphore()
    ingest_copy = pltpu.make_async_copy(ingest_hbm, ingest_ref, ingest_sem)
    ingest_copy.start()
    local_copies = [pltpu.make_async_copy(src, dst, local_sems.at[i]) for i, (src, dst) in enumerate((
        (shard_hbm, shard_ref), (slot_hbm, slot_ref), (hist_hbm, hist_ref), (w_hbm, w_ref)))]
    for copy in local_copies:
        copy.start()
    for axis, me, count in (("ctx", my_ctx, ctxs), ("head", my_head, heads)):
        for offset in range(1, count):
            pl.semaphore_signal(barrier, inc=1, device_id={axis: lax.rem(me + offset, count)}, device_id_type=MESH)
    has_low, has_high = my_group > 0, my_group < groups - 1

    def tell(there, semaphore, to):
        @pl.when(there)
        def _():
            pl.semaphore_signal(semaphore, inc=1, device_id={"batch": to}, device_id_type=MESH)

    tell(has_low, barrier, my_group - 1)
    tell(has_high, barrier, my_group + 1)
    neighbours = jnp.where(has_low, 1, 0) + jnp.where(has_high, 1, 0)

    for copy in local_copies:
        copy.wait()
    slots = []
    for dst in range(groups):
        picked = [jnp.int32(0)] * capacity
        seen = jnp.int32(0)
        for j in range(per_owner):
            hit = shard_ref[dst, j] == my_group
            slot = slot_ref[dst, j]
            for k in range(capacity):
                picked[k] = jnp.where(hit & (seen == k), slot, picked[k])
            seen = seen + jnp.where(hit, 1, 0)
        slots.append(picked)

    sources = [shard_ref[my_group, j] for j in range(per_owner)]
    ranks, sides = [], []
    for j in range(per_owner):
        rank = jnp.int32(0)
        for i in range(j):
            rank = rank + jnp.where(sources[i] == sources[j], 1, 0)
        ranks.append(jnp.minimum(rank, capacity - 1))
        sides.append(jnp.where(sources[j] == sources[0], 0, 1))

    def split_kind(kind):
        width = 4 * rows
        row = lax.broadcasted_iota(jnp.int32, (rows, width), 0)
        col = lax.broadcasted_iota(jnp.int32, (rows, width), 1)
        pick = jnp.where(col == row * 4 + kind, 1.0, 0.0).astype(jnp.bfloat16)

        def one(dst, k):
            block = ingest_ref[slots[dst][k]]
            return jnp.dot(pick, block, preferred_element_type=jnp.float32).astype(jnp.bfloat16)

        return one

    masks = list(range(groups - 1, 0, -1))
    peers = {m: partner(my_group, m, groups) for m in masks}

    def fill(kind):
        one = split_kind(kind)
        for dst in range(groups):
            for k in range(capacity):
                if kind == UPDATE:
                    block = one(dst, k)
                    for c, (of, low, size) in enumerate(chunks):
                        if of == k:
                            send_u[c][dst] = block[low:low + size]
                else:
                    send_bufs[FIRST_KINDS.index(kind), dst, k] = one(dst, k)

    copies = {}

    def send(kind):
        if kind == UPDATE:
            for c in range(len(chunks)):
                for m in masks:
                    copies[kind, c, m] = pltpu.make_async_remote_copy(
                        src_ref=send_u[c].at[peers[m]], dst_ref=recv_u[c].at[my_group],
                        send_sem=u_send.at[c, m], recv_sem=u_recv.at[c, m],
                        device_id={"batch": peers[m]}, device_id_type=MESH)
                    copies[kind, c, m].start()
                recv_u[c][my_group] = send_u[c][my_group]
            return
        n = FIRST_KINDS.index(kind)
        for m in masks:
            copies[kind, m] = pltpu.make_async_remote_copy(
                src_ref=send_bufs.at[n, peers[m]], dst_ref=recv_bufs[n].at[my_group],
                send_sem=z_send.at[n, m], recv_sem=z_recv.at[n, m],
                device_id={"batch": peers[m]}, device_id_type=MESH)
            if kind != KEY:
                copies[kind, m].start()
        recv_bufs[n][my_group] = send_bufs[n, my_group]

    def collect(kind, own_ref):
        n = FIRST_KINDS.index(kind)
        for m in masks:
            copies[kind, m].wait()
        for j in range(per_owner):
            own_ref[j * rows:(j + 1) * rows, :] = recv_bufs[n][sources[j], ranks[j]]

    def start_at(distance):
        for m in masks:
            @pl.when((peers[m] - my_group == distance) | (my_group - peers[m] == distance))
            def _():
                copies[KEY, m].start()

    def hear(distance):
        for there, semaphore in ((my_group >= distance, from_low), (my_group + distance < groups, from_high)):
            @pl.when(there)
            def _():
                pl.semaphore_wait(semaphore.at[distance], 1)

    def pass_on(distance):
        tell((my_group >= distance) & has_high, from_low.at[distance + 1], my_group + 1)
        tell((my_group + distance < groups) & has_low, from_high.at[distance + 1], my_group - 1)

    ingest_copy.wait()
    fill(KEY)
    pl.semaphore_wait(barrier, neighbours + ctxs + heads - 2)
    if groups > 2:
        pass_on(1)
    send(KEY)
    start_at(1)
    fill(VALUE)
    for distance in range(2, groups):
        hear(distance)
        if distance + 1 < groups:
            pass_on(distance)
        start_at(distance)
    send(VALUE)
    fill(QUERY)
    send(QUERY)
    fill(UPDATE)
    send(UPDATE)

    w_copies = []
    for offset in range(1, heads):
        to = lax.rem(my_head + offset, heads)
        copy = pltpu.make_async_remote_copy(
            src_ref=w_ref.at[:, pl.ds(pl.multiple_of(to * HD, HD), HD)], dst_ref=w_cols.at[my_head],
            send_sem=w_send.at[offset], recv_sem=w_recv.at[offset],
            device_id={"head": to}, device_id_type=MESH)
        copy.start()
        w_copies.append(copy)
    w_cols[my_head] = w_ref[:, pl.ds(pl.multiple_of(my_head * HD, HD), HD)]

    ends, total = [], jnp.int32(0)
    for u in range(hist_ref.shape[0]):
        total = total + hist_ref[u]
        ends.append(total)
    base = my_ctx * row_count
    position = base + lax.broadcasted_iota(jnp.int32, (row_count, HD), 0)
    first = jnp.zeros((row_count, HD), jnp.int32)
    for end in ends:
        first = jnp.where(position >= end, end, first)
    start_ref[...] = first - base

    def ctx_copy(n, own_ref, prev_ref, offset):
        return pltpu.make_async_remote_copy(
            src_ref=own_ref, dst_ref=prev_ref.at[offset - 1],
            send_sem=c_send.at[n, offset - 1], recv_sem=c_recv.at[n, offset - 1],
            device_id={"ctx": lax.rem(my_ctx + offset, ctxs)}, device_id_type=MESH)

    def push(n, own_ref, prev_ref):
        for offset in range(1, window + 1):
            @pl.when(my_ctx + offset < ctxs)
            def _():
                ctx_copy(n, own_ref, prev_ref, offset).start()

    collect(KEY, own_k)
    push(0, own_k, prev_k)
    collect(VALUE, own_v)
    push(1, own_v, prev_v)
    collect(QUERY, own_q)

    tile = 2 * rows if per_owner % 2 == 0 else rows
    tiles = row_count // tile
    half_scale = 0.5 / math.sqrt(HD)

    def attend(q, key_tile, value_tile, q_lo, k_lo, shift, causal):
        scores = lax.dot_general(q, key_tile, (((1,), (1,)), ((), ())), preferred_element_type=jnp.float32)
        half = scores * half_scale
        act = half + half * jnp.tanh(half)
        key_pos = lax.broadcasted_iota(jnp.int32, (tile, tile), 1) + (k_lo - shift)
        first_pos = jnp.concatenate([start_ref[q_lo:q_lo + tile, :]] * (tile // HD), axis=1)
        visible = key_pos >= first_pos
        if causal:
            visible = visible & (key_pos <= lax.broadcasted_iota(jnp.int32, (tile, tile), 0) + q_lo)
        weights = jnp.where(visible, act, 0.0).astype(jnp.bfloat16)
        return jnp.dot(weights, value_tile, preferred_element_type=jnp.float32)

    def put(i, value, add):
        for part in range(tile // rows):
            at = i * (tile // rows) + part
            piece = value[part * rows:(part + 1) * rows]
            att[at] = att[at] + piece if add else piece

    for i in range(tiles):
        q = own_q[i * tile:(i + 1) * tile, :]
        acc = None
        for t in range(i + 1):
            span = slice(t * tile, (t + 1) * tile)
            term = attend(q, own_k[span, :], own_v[span, :], i * tile, t * tile, 0, t == i)
            acc = term if acc is None else acc + term
        put(i, acc, False)
    for offset in range(1, window + 1):
        @pl.when(my_ctx >= offset)
        def _():
            ctx_copy(0, own_k, prev_k, offset).wait_recv()
            ctx_copy(1, own_v, prev_v, offset).wait_recv()
            for i in range(tiles):
                q = own_q[i * tile:(i + 1) * tile, :]
                acc = None
                for t in range(i if offset == window else 0, tiles):
                    span = slice(t * tile, (t + 1) * tile)
                    term = attend(q, prev_k[offset - 1, span, :], prev_v[offset - 1, span, :],
                                  i * tile, t * tile, offset * row_count, False)
                    acc = term if acc is None else acc + term
                put(i, acc, True)

    source_other = sources[0]
    for j in range(1, per_owner):
        source_other = jnp.where(sides[j] == 1, sources[j], source_other)
    side_source = (sources[0], source_other)
    h_copies = []
    for c, (k, low, size) in enumerate(chunks):
        for m in masks:
            copies[UPDATE, c, m].wait()
        for side in range(2):
            at = jnp.int32(0)
            for j in range(per_owner):
                at = jnp.where((ranks[j] == k) & (sides[j] == side), j, at)
            rows_f32 = att[at, low:low + size, :]
            mean_square = jnp.mean(rows_f32 * rows_f32, axis=-1, keepdims=True)
            normed = rows_f32 * lax.rsqrt(mean_square + 1e-06)
            update = recv_u[c][side_source[side]].astype(jnp.float32)
            gated[c][my_head, side * size:(side + 1) * size, :] = (normed * update).astype(jnp.bfloat16)
        for offset in range(1, heads):
            copy = pltpu.make_async_remote_copy(
                src_ref=gated[c].at[my_head], dst_ref=gated[c].at[my_head],
                send_sem=h_send.at[c, offset], recv_sem=h_recv.at[c, offset],
                device_id={"head": lax.rem(my_head + offset, heads)}, device_id_type=MESH)
            copy.start()
            h_copies.append(copy)
    for copy in w_copies:
        copy.wait()
    for c, (k, low, size) in enumerate(chunks):
        for copy in h_copies[c * (heads - 1):(c + 1) * (heads - 1)]:
            copy.wait()
        acc = None
        for h in range(heads):
            term = jnp.dot(gated[c][h], w_cols[h], preferred_element_type=jnp.float32)
            acc = term if acc is None else acc + term
        acc = acc.astype(jnp.bfloat16)
        for side in range(2):
            mixed[2 * k + side, low:low + size, :] = acc[side * size:(side + 1) * size]
    for j in range(per_owner):
        out_ref[j * rows:(j + 1) * rows, :] = mixed[2 * ranks[j] + sides[j]]
    for offset in range(1, window + 1):
        @pl.when(my_ctx + offset < ctxs)
        def _():
            ctx_copy(0, own_k, prev_k, offset).wait_send()
            ctx_copy(1, own_v, prev_v, offset).wait_send()


def body(ingest, src_shard, src_slot, hist_len, w_out):
    groups, ctxs, heads = (lax.axis_size(a) for a in ("batch", "ctx", "head"))
    slot_total, rows, kinds, width = ingest.shape[2:]
    per_owner = src_shard.shape[2]
    capacity = per_owner // 2
    chunks = update_chunks(capacity, rows)
    window = ctxs // 2
    row_count = per_owner * rows
    bf16 = jnp.bfloat16
    dma = pltpu.SemaphoreType.DMA
    vmem = pl.BlockSpec(memory_space=pltpu.VMEM)
    mixed = pl.pallas_call(
        functools.partial(kernel, (groups, ctxs, heads, per_owner, rows)),
        out_shape=pltpu.VMEM((row_count, width), bf16),
        in_specs=[pl.BlockSpec(memory_space=pl.ANY)] * 5,
        out_specs=vmem,
        scratch_shapes=[
            pltpu.SMEM(src_shard.shape[1:], jnp.int32), pltpu.SMEM(src_slot.shape[1:], jnp.int32),
            pltpu.SMEM(hist_len.shape[1:], jnp.int32), pltpu.VMEM(w_out.shape, bf16), dma((4,)),
            pltpu.VMEM((slot_total, rows * kinds, width), bf16),
            pltpu.VMEM((3, groups, capacity, rows, width), bf16),
            [pltpu.VMEM((groups, size, width), bf16) for _, _, size in chunks],
            [pltpu.VMEM((groups, capacity, rows, width), bf16)] * 3,
            [pltpu.VMEM((groups, size, width), bf16) for _, _, size in chunks],
            pltpu.VMEM((row_count, width), bf16),
            pltpu.VMEM((row_count, width), bf16),
            pltpu.VMEM((row_count, width), bf16),
            pltpu.VMEM((window, row_count, width), bf16),
            pltpu.VMEM((window, row_count, width), bf16),
            pltpu.VMEM((row_count, width), jnp.int32),
            pltpu.VMEM((per_owner, rows, width), jnp.float32),
            [pltpu.VMEM((heads, 2 * size, width), bf16) for _, _, size in chunks],
            pltpu.VMEM((heads, width, width), bf16),
            pltpu.VMEM((per_owner, rows, width), bf16),
            dma((3, groups)), dma((3, groups)),
            dma((len(chunks), groups)), dma((len(chunks), groups)),
            dma((2, window)), dma((2, window)),
            dma((len(chunks), heads)), dma((len(chunks), heads)),
            dma((heads,)), dma((heads,)),
            dma, pltpu.SemaphoreType.REGULAR((groups,)), pltpu.SemaphoreType.REGULAR((groups,)),
        ],
        compiler_params=pltpu.CompilerParams(
            collective_id=0, has_side_effects=True, vmem_limit_bytes=56 * 1024 * 1024),
    )(src_shard[0], src_slot[0], hist_len[0],
      ingest.reshape(slot_total, rows * kinds, width), w_out)
    return mixed[None]


def solution(mesh):
    in_specs = (
        P("ctx", "batch", None, None, None, "head"),
        P("ctx", None, None),
        P("ctx", None, None),
        P("batch", None),
        P("head", None),
    )
    out_specs = P("batch", "ctx", "head")
    return jax.shard_map(body, mesh=mesh, in_specs=in_specs, out_specs=out_specs, check_vma=False)
```

```python
import functools
import math

import jax
import jax.numpy as jnp
from jax import lax
from jax.experimental import pallas as pl
from jax.experimental.pallas import tpu as pltpu
from jax.sharding import PartitionSpec as P

HD = 128
MESH = pl.DeviceIdType.MESH
QUERY, KEY, VALUE, UPDATE = 0, 1, 2, 3
FIRST_KINDS = (KEY, VALUE, QUERY)


def partner(me, mask, count):
    out = 0
    bit = 1
    while bit < count:
        out = out + lax.rem(lax.div(me, bit) + (mask // bit) % 2, 2) * bit
        bit *= 2
    return out


def update_chunks(capacity, rows):
    half = rows // 2
    return [(k, 0, rows) for k in range(capacity - 1)] + [(capacity - 1, 0, half), (capacity - 1, half, half)]


def kernel(sizes, shard_hbm, slot_hbm, hist_hbm, ingest_hbm, w_hbm, out_ref,
           shard_ref, slot_ref, hist_ref, w_ref, local_sems,
           ingest_ref,
           send_bufs, send_u, recv_bufs, recv_u, own_k, own_v, own_q, prev_k, prev_v,
           start_ref, att, gated, w_cols, mixed,
           z_send, z_recv, u_send, u_recv, c_send, c_recv, h_send, h_recv, w_send, w_recv,
           ingest_sem, from_low, from_high):
    groups, ctxs, heads, per_owner, rows = sizes
    capacity = per_owner // 2
    chunks = update_chunks(capacity, rows)
    window = ctxs // 2
    row_count = per_owner * rows
    my_group = lax.axis_index("batch")
    my_ctx = lax.axis_index("ctx")
    my_head = lax.axis_index("head")

    barrier = pltpu.get_barrier_semaphore()
    ingest_copy = pltpu.make_async_copy(ingest_hbm, ingest_ref, ingest_sem)
    ingest_copy.start()
    local_copies = [pltpu.make_async_copy(src, dst, local_sems.at[i]) for i, (src, dst) in enumerate((
        (shard_hbm, shard_ref), (slot_hbm, slot_ref), (hist_hbm, hist_ref), (w_hbm, w_ref)))]
    for copy in local_copies:
        copy.start()
    for axis, me, count in (("ctx", my_ctx, ctxs), ("head", my_head, heads)):
        for offset in range(1, count):
            pl.semaphore_signal(barrier, inc=1, device_id={axis: lax.rem(me + offset, count)}, device_id_type=MESH)
    has_low, has_high = my_group > 0, my_group < groups - 1

    def tell(there, semaphore, to):
        @pl.when(there)
        def _():
            pl.semaphore_signal(semaphore, inc=1, device_id={"batch": to}, device_id_type=MESH)

    tell(has_low, barrier, my_group - 1)
    tell(has_high, barrier, my_group + 1)
    neighbours = jnp.where(has_low, 1, 0) + jnp.where(has_high, 1, 0)

    for copy in local_copies:
        copy.wait()
    slots = []
    for dst in range(groups):
        picked = [jnp.int32(0)] * capacity
        seen = jnp.int32(0)
        for j in range(per_owner):
            hit = shard_ref[dst, j] == my_group
            slot = slot_ref[dst, j]
            for k in range(capacity):
                picked[k] = jnp.where(hit & (seen == k), slot, picked[k])
            seen = seen + jnp.where(hit, 1, 0)
        slots.append(picked)

    sources = [shard_ref[my_group, j] for j in range(per_owner)]
    ranks, sides = [], []
    for j in range(per_owner):
        rank = jnp.int32(0)
        for i in range(j):
            rank = rank + jnp.where(sources[i] == sources[j], 1, 0)
        ranks.append(jnp.minimum(rank, capacity - 1))
        sides.append(jnp.where(sources[j] == sources[0], 0, 1))

    def split_kind(kind):
        width = 4 * rows
        row = lax.broadcasted_iota(jnp.int32, (rows, width), 0)
        col = lax.broadcasted_iota(jnp.int32, (rows, width), 1)
        pick = jnp.where(col == row * 4 + kind, 1.0, 0.0).astype(jnp.bfloat16)

        def one(dst, k):
            block = ingest_ref[slots[dst][k]]
            return jnp.dot(pick, block, preferred_element_type=jnp.float32).astype(jnp.bfloat16)

        return one

    masks = list(range(groups - 1, 0, -1))
    peers = {m: partner(my_group, m, groups) for m in masks}

    def fill(kind):
        one = split_kind(kind)
        for dst in range(groups):
            for k in range(capacity):
                if kind == UPDATE:
                    block = one(dst, k)
                    for c, (of, low, size) in enumerate(chunks):
                        if of == k:
                            send_u[c][dst] = block[low:low + size]
                else:
                    send_bufs[FIRST_KINDS.index(kind), dst, k] = one(dst, k)

    copies = {}

    def send(kind):
        if kind == UPDATE:
            for c in range(len(chunks)):
                for m in masks:
                    copies[kind, c, m] = pltpu.make_async_remote_copy(
                        src_ref=send_u[c].at[peers[m]], dst_ref=recv_u[c].at[my_group],
                        send_sem=u_send.at[c, m], recv_sem=u_recv.at[c, m],
                        device_id={"batch": peers[m]}, device_id_type=MESH)
                    copies[kind, c, m].start()
                recv_u[c][my_group] = send_u[c][my_group]
            return
        n = FIRST_KINDS.index(kind)
        for m in masks:
            copies[kind, m] = pltpu.make_async_remote_copy(
                src_ref=send_bufs.at[n, peers[m]], dst_ref=recv_bufs[n].at[my_group],
                send_sem=z_send.at[n, m], recv_sem=z_recv.at[n, m],
                device_id={"batch": peers[m]}, device_id_type=MESH)
            if kind != KEY:
                copies[kind, m].start()
        recv_bufs[n][my_group] = send_bufs[n, my_group]

    def collect(kind, own_ref):
        n = FIRST_KINDS.index(kind)
        for m in masks:
            copies[kind, m].wait()
        for j in range(per_owner):
            own_ref[j * rows:(j + 1) * rows, :] = recv_bufs[n][sources[j], ranks[j]]

    def start_at(distance):
        for m in masks:
            @pl.when((peers[m] - my_group == distance) | (my_group - peers[m] == distance))
            def _():
                copies[KEY, m].start()

    def hear(distance):
        for there, semaphore in ((my_group >= distance, from_low), (my_group + distance < groups, from_high)):
            @pl.when(there)
            def _():
                pl.semaphore_wait(semaphore.at[distance], 1)

    def pass_on(distance):
        tell((my_group >= distance) & has_high, from_low.at[distance + 1], my_group + 1)
        tell((my_group + distance < groups) & has_low, from_high.at[distance + 1], my_group - 1)

    ingest_copy.wait()
    fill(KEY)
    pl.semaphore_wait(barrier, neighbours + ctxs + heads - 2)
    if groups > 2:
        pass_on(1)
    send(KEY)
    start_at(1)
    fill(VALUE)
    for distance in range(2, groups):
        hear(distance)
        if distance + 1 < groups:
            pass_on(distance)
        start_at(distance)
    send(VALUE)
    fill(QUERY)
    send(QUERY)
    fill(UPDATE)
    send(UPDATE)

    w_copies = []
    for offset in range(1, heads):
        to = lax.rem(my_head + offset, heads)
        copy = pltpu.make_async_remote_copy(
            src_ref=w_ref.at[:, pl.ds(pl.multiple_of(to * HD, HD), HD)], dst_ref=w_cols.at[my_head],
            send_sem=w_send.at[offset], recv_sem=w_recv.at[offset],
            device_id={"head": to}, device_id_type=MESH)
        copy.start()
        w_copies.append(copy)
    w_cols[my_head] = w_ref[:, pl.ds(pl.multiple_of(my_head * HD, HD), HD)]

    ends, total = [], jnp.int32(0)
    for u in range(hist_ref.shape[0]):
        total = total + hist_ref[u]
        ends.append(total)
    base = my_ctx * row_count
    position = base + lax.broadcasted_iota(jnp.int32, (row_count, HD), 0)
    first = jnp.zeros((row_count, HD), jnp.int32)
    for end in ends:
        first = jnp.where(position >= end, end, first)
    start_ref[...] = first - base

    def ctx_copy(n, own_ref, prev_ref, offset):
        return pltpu.make_async_remote_copy(
            src_ref=own_ref, dst_ref=prev_ref.at[offset - 1],
            send_sem=c_send.at[n, offset - 1], recv_sem=c_recv.at[n, offset - 1],
            device_id={"ctx": lax.rem(my_ctx + offset, ctxs)}, device_id_type=MESH)

    def push(n, own_ref, prev_ref):
        for offset in range(1, window + 1):
            @pl.when(my_ctx + offset < ctxs)
            def _():
                ctx_copy(n, own_ref, prev_ref, offset).start()

    collect(KEY, own_k)
    push(0, own_k, prev_k)
    collect(VALUE, own_v)
    push(1, own_v, prev_v)
    collect(QUERY, own_q)

    tile = 2 * rows if per_owner % 2 == 0 else rows
    tiles = row_count // tile
    half_scale = 0.5 / math.sqrt(HD)

    def attend(q, key_tile, value_tile, q_lo, k_lo, shift, causal):
        scores = lax.dot_general(q, key_tile, (((1,), (1,)), ((), ())), preferred_element_type=jnp.float32)
        half = scores * half_scale
        act = half + half * jnp.tanh(half)
        key_pos = lax.broadcasted_iota(jnp.int32, (tile, tile), 1) + (k_lo - shift)
        first_pos = jnp.concatenate([start_ref[q_lo:q_lo + tile, :]] * (tile // HD), axis=1)
        visible = key_pos >= first_pos
        if causal:
            visible = visible & (key_pos <= lax.broadcasted_iota(jnp.int32, (tile, tile), 0) + q_lo)
        weights = jnp.where(visible, act, 0.0).astype(jnp.bfloat16)
        return jnp.dot(weights, value_tile, preferred_element_type=jnp.float32)

    def put(i, value, add):
        for part in range(tile // rows):
            at = i * (tile // rows) + part
            piece = value[part * rows:(part + 1) * rows]
            att[at] = att[at] + piece if add else piece

    for i in range(tiles):
        q = own_q[i * tile:(i + 1) * tile, :]
        acc = None
        for t in range(i + 1):
            span = slice(t * tile, (t + 1) * tile)
            term = attend(q, own_k[span, :], own_v[span, :], i * tile, t * tile, 0, t == i)
            acc = term if acc is None else acc + term
        put(i, acc, False)
    for offset in range(1, window + 1):
        @pl.when(my_ctx >= offset)
        def _():
            ctx_copy(0, own_k, prev_k, offset).wait_recv()
            ctx_copy(1, own_v, prev_v, offset).wait_recv()
            for i in range(tiles):
                q = own_q[i * tile:(i + 1) * tile, :]
                acc = None
                for t in range(i if offset == window else 0, tiles):
                    span = slice(t * tile, (t + 1) * tile)
                    term = attend(q, prev_k[offset - 1, span, :], prev_v[offset - 1, span, :],
                                  i * tile, t * tile, offset * row_count, False)
                    acc = term if acc is None else acc + term
                put(i, acc, True)

    source_other = sources[0]
    for j in range(1, per_owner):
        source_other = jnp.where(sides[j] == 1, sources[j], source_other)
    side_source = (sources[0], source_other)
    for j in range(per_owner):
        rows_f32 = att[j]
        mean_square = jnp.mean(rows_f32 * rows_f32, axis=-1, keepdims=True)
        att[j] = rows_f32 * lax.rsqrt(mean_square + 1e-06)
    h_copies = []
    for c, (k, low, size) in enumerate(chunks):
        for m in masks:
            copies[UPDATE, c, m].wait()
        for side in range(2):
            at = jnp.int32(0)
            for j in range(per_owner):
                at = jnp.where((ranks[j] == k) & (sides[j] == side), j, at)
            normed = att[at, low:low + size, :]
            update = recv_u[c][side_source[side]].astype(jnp.float32)
            gated[c][my_head, side * size:(side + 1) * size, :] = (normed * update).astype(jnp.bfloat16)
        for offset in range(1, heads):
            copy = pltpu.make_async_remote_copy(
                src_ref=gated[c].at[my_head], dst_ref=gated[c].at[my_head],
                send_sem=h_send.at[c, offset], recv_sem=h_recv.at[c, offset],
                device_id={"head": lax.rem(my_head + offset, heads)}, device_id_type=MESH)
            copy.start()
            h_copies.append(copy)
    for copy in w_copies:
        copy.wait()
    for c, (k, low, size) in enumerate(chunks):
        for copy in h_copies[c * (heads - 1):(c + 1) * (heads - 1)]:
            copy.wait()
        acc = None
        for h in range(heads):
            term = jnp.dot(gated[c][h], w_cols[h], preferred_element_type=jnp.float32)
            acc = term if acc is None else acc + term
        acc = acc.astype(jnp.bfloat16)
        for side in range(2):
            mixed[2 * k + side, low:low + size, :] = acc[side * size:(side + 1) * size]
    for j in range(per_owner):
        out_ref[j * rows:(j + 1) * rows, :] = mixed[2 * ranks[j] + sides[j]]
    for offset in range(1, window + 1):
        @pl.when(my_ctx + offset < ctxs)
        def _():
            ctx_copy(0, own_k, prev_k, offset).wait_send()
            ctx_copy(1, own_v, prev_v, offset).wait_send()


def body(ingest, src_shard, src_slot, hist_len, w_out):
    groups, ctxs, heads = (lax.axis_size(a) for a in ("batch", "ctx", "head"))
    slot_total, rows, kinds, width = ingest.shape[2:]
    per_owner = src_shard.shape[2]
    capacity = per_owner // 2
    chunks = update_chunks(capacity, rows)
    window = ctxs // 2
    row_count = per_owner * rows
    bf16 = jnp.bfloat16
    dma = pltpu.SemaphoreType.DMA
    vmem = pl.BlockSpec(memory_space=pltpu.VMEM)
    mixed = pl.pallas_call(
        functools.partial(kernel, (groups, ctxs, heads, per_owner, rows)),
        out_shape=pltpu.VMEM((row_count, width), bf16),
        in_specs=[pl.BlockSpec(memory_space=pl.ANY)] * 5,
        out_specs=vmem,
        scratch_shapes=[
            pltpu.SMEM(src_shard.shape[1:], jnp.int32), pltpu.SMEM(src_slot.shape[1:], jnp.int32),
            pltpu.SMEM(hist_len.shape[1:], jnp.int32), pltpu.VMEM(w_out.shape, bf16), dma((4,)),
            pltpu.VMEM((slot_total, rows * kinds, width), bf16),
            pltpu.VMEM((3, groups, capacity, rows, width), bf16),
            [pltpu.VMEM((groups, size, width), bf16) for _, _, size in chunks],
            [pltpu.VMEM((groups, capacity, rows, width), bf16)] * 3,
            [pltpu.VMEM((groups, size, width), bf16) for _, _, size in chunks],
            pltpu.VMEM((row_count, width), bf16),
            pltpu.VMEM((row_count, width), bf16),
            pltpu.VMEM((row_count, width), bf16),
            pltpu.VMEM((window, row_count, width), bf16),
            pltpu.VMEM((window, row_count, width), bf16),
            pltpu.VMEM((row_count, width), jnp.int32),
            pltpu.VMEM((per_owner, rows, width), jnp.float32),
            [pltpu.VMEM((heads, 2 * size, width), bf16) for _, _, size in chunks],
            pltpu.VMEM((heads, width, width), bf16),
            pltpu.VMEM((per_owner, rows, width), bf16),
            dma((3, groups)), dma((3, groups)),
            dma((len(chunks), groups)), dma((len(chunks), groups)),
            dma((2, window)), dma((2, window)),
            dma((len(chunks), heads)), dma((len(chunks), heads)),
            dma((heads,)), dma((heads,)),
            dma, pltpu.SemaphoreType.REGULAR((groups,)), pltpu.SemaphoreType.REGULAR((groups,)),
        ],
        compiler_params=pltpu.CompilerParams(
            collective_id=0, has_side_effects=True, vmem_limit_bytes=56 * 1024 * 1024),
    )(src_shard[0], src_slot[0], hist_len[0],
      ingest.reshape(slot_total, rows * kinds, width), w_out)
    return mixed[None]


def solution(mesh):
    in_specs = (
        P("ctx", "batch", None, None, None, "head"),
        P("ctx", None, None),
        P("ctx", None, None),
        P("batch", None),
        P("head", None),
    )
    out_specs = P("batch", "ctx", "head")
    return jax.shard_map(body, mesh=mesh, in_specs=in_specs, out_specs=out_specs, check_vma=False)
```
